32 devices in a mesh: rows: 2 (over core), tp: 4 (over y, x), attn: 4 (over z).
Axes of the slice: x: 2, y: 2, z: 4, core: 2. Of those that a mesh axis runs over, the one named last changes fastest.
Arguments:
- tokens: bfloat16 [4096, 4096], P(('rows', 'attn')), may hold values from -60 to 60, as said below
- norm_gain: bfloat16 [4096], replicated, may hold values from 0.099609375 to 1.8984375
- w_query: bfloat16 [4096, 2048], P('rows', 'tp'), may hold values from -1 to 1, as said below
- key_projection_weight: bfloat16 [4096, 512], P('rows', 'tp'), may hold values from -8 to 8, as said below
- value_projection_weight: bfloat16 [4096, 512], P('rows', 'tp'), may hold values from -0.09375 to 0.09375
- documents: int32 [2, 2048], P('rows'), may hold values from 0 to 5, never falling along the last dimension, each value on 1 to 1024 neighbouring positions
Outputs:
- attn_out: bfloat16 [4096, 2048], P(('rows', 'attn'), 'tp')
The draws below stay inside these ranges and needn't reach their ends.
Inputs may be any that keep to these rules, and one draw needn't show every extreme that they name: `tokens`: activations of order one. `w_query`: entries of order 4096 ** -0.5. `key_projection_weight`: entries of order one or smaller. `documents`: along each window the document numbers never fall; every document spans 1 to 1024 tokens and some document of each window spans exactly 1024.
All inputs are finite; a program needn't handle non-finite values.
Results may differ from the reference program's by a relative error of at most 0.012.
The reference program's roundings to bfloat16 on the way count: a program that leaves them out, or rounds other values in their place, can miss the bound.
Values may be sent and summed in bfloat16 or wider, within the bound.
A program may use at most 64 MiB of HBM per device.

```python
import math
import jax
import jax.numpy as jnp
import numpy as np
from jax import lax

MODEL_WIDTH = 4096
QUERY_HEADS = 16
KEY_VALUE_HEADS = 4
HEAD_SIZE = 128
DOCS = 6
WINDOW_TOKENS = 2048
MOST = 1024
TOKENS = 4096
N_ROWS = 2


def draw_tokens(key, part):
    base = jax.random.normal(jax.random.fold_in(key, 11), (TOKENS, MODEL_WIDTH), jnp.float32)
    row_scale = jnp.exp(jax.random.uniform(jax.random.fold_in(key, 12), (TOKENS, 1), jnp.float32, math.log(0.3), math.log(3.0)))
    column_scale = jnp.exp(jax.random.uniform(jax.random.fold_in(key, 13), (1, MODEL_WIDTH), jnp.float32, math.log(0.3), math.log(3.0)))
    return jnp.clip(base * row_scale * column_scale, -60.0, 60.0).astype(jnp.bfloat16)


def projection_pair(key):
    query_matrix = jax.random.normal(jax.random.fold_in(key, 21), (MODEL_WIDTH, QUERY_HEADS * HEAD_SIZE), jnp.float32) * MODEL_WIDTH ** (-0.5)
    key_matrix = jax.random.normal(jax.random.fold_in(key, 22), (MODEL_WIDTH, KEY_VALUE_HEADS * HEAD_SIZE), jnp.float32) * MODEL_WIDTH ** (-0.5)
    return (jnp.clip(query_matrix, -1.0, 1.0), jnp.clip(key_matrix, -8.0, 8.0))


def draw_w_query(key, part):
    return projection_pair(key)[0].astype(jnp.bfloat16)


def draw_key_projection_weight(key, part):
    return projection_pair(key)[1].astype(jnp.bfloat16)


def block_scale(stream_key, extent, shards, smallest, high):
    level = 1.0
    for axis_at, blocks in shards:
        draws = jax.random.uniform(jax.random.fold_in(jax.random.fold_in(stream_key, 6), axis_at), (blocks,), jnp.float32, smallest / len(shards), high / len(shards))
        level = level * jnp.repeat(jnp.exp(draws), extent[axis_at] // blocks).reshape((-1,) + (1,) * (len(extent) - 1 - axis_at))
    return level


def length_profile(amount, total, limit, skew):
    loads = [(1 << 20) // math.isqrt(standing ** skew) + 1 for standing in range(2, amount + 1)]
    spare, given = total - limit - (amount - 1), [1] * (amount - 1)
    while spare > 0:
        movable = [i for i in range(amount - 1) if given[i] < limit]
        mass, left = sum([loads[i] for i in movable]), spare
        for i in movable:
            more = min(limit - given[i], max(1, left * loads[i] // mass), spare)
            given[i] = given[i] + more
            spare = spare - more
    return np.array([limit] + given)


def ragged_sizes(stream_key, count, total, most, lean):
    if count == 2:
        one = jax.random.randint(stream_key, (), max(1, total - most), min(most, total - 1) + 1)
        return jnp.stack([one, total - one])
    lengths = jnp.asarray(length_profile(count, total, most, lean), jnp.int32)
    pairs = (count - 1) // 2
    source_of, receiver = lengths[1:1 + 2 * pairs:2], lengths[2:2 + 2 * pairs:2]
    margin = jnp.minimum(source_of - 1, most - receiver)
    shifted = jax.random.randint(jax.random.fold_in(stream_key, 1), (pairs,), 0, 1 << 20) % (margin + 1)
    lengths = lengths.at[1:1 + 2 * pairs:2].set(source_of - shifted).at[2:2 + 2 * pairs:2].set(receiver + shifted)
    return lengths[jax.random.permutation(jax.random.fold_in(stream_key, 2), count)]


def gaussian(own_key, shape, scale, limit, pieces=(), kind=jnp.bfloat16):
    result = jax.random.normal(own_key, shape, jnp.float32) * scale
    if len(pieces) > 0:
        result = block_scale(own_key, shape, pieces, -0.22, 0.18) * result
    return jnp.clip(result, min=-limit, max=limit).astype(kind)


def setup_inputs(seed: int = 0) -> dict:
    streams_of = jax.random.split(jax.random.key(seed), 7)
    tokens = draw_tokens(jax.random.fold_in(streams_of[6], 71), 0)
    norm_gain = jnp.clip(1.0 + 0.18 * jax.random.normal(streams_of[1], (MODEL_WIDTH,), jnp.float32), 0.099609375, 1.8984375).astype(jnp.bfloat16)
    w_query = draw_w_query(jax.random.fold_in(streams_of[6], 71), 0)
    key_projection_weight = draw_key_projection_weight(jax.random.fold_in(streams_of[6], 71), 0)
    value_projection_weight = gaussian(streams_of[4], (MODEL_WIDTH, KEY_VALUE_HEADS * HEAD_SIZE), MODEL_WIDTH ** -0.5, 0.09375, ((0, 2), (1, 4)))
    documents = jax.vmap(lambda own: jnp.searchsorted(jnp.cumsum(ragged_sizes(own, DOCS, WINDOW_TOKENS, MOST, 2)), jnp.arange(WINDOW_TOKENS), side="right"))(jax.random.split(streams_of[5], N_ROWS)).reshape((N_ROWS, WINDOW_TOKENS)).astype(jnp.int32)
    return {"tokens": tokens, "norm_gain": norm_gain, "w_query": w_query, "key_projection_weight": key_projection_weight, "value_projection_weight": value_projection_weight, "documents": documents}


def rotary(vectors, positions):
    head_dim = vectors.shape[-1]
    half_dim = head_dim // 2
    frequency = jnp.exp(jnp.arange(half_dim, dtype=jnp.float32) * (-2.0 * math.log(500000.0) / head_dim))
    angles = positions.astype(jnp.float32)[:, None] * frequency[None, :]
    cosine_table = jnp.cos(angles)[:, None, :]
    sine_table = jnp.sin(angles)[:, None, :]
    first_half = vectors[..., :half_dim]
    second_half = vectors[..., half_dim:]
    return jnp.concatenate([first_half * cosine_table - second_half * sine_table, second_half * cosine_table + first_half * sine_table], axis=-1)

def rms_normed(tokens, norm_gain):
    widened = tokens.astype(jnp.float32)
    mean_sq = lax.optimization_barrier(jnp.mean(widened * widened, axis=-1, keepdims=True))
    return (widened * lax.rsqrt(mean_sq + 1e-05) * norm_gain.astype(jnp.float32)).astype(jnp.bfloat16)

def reference(tokens, norm_gain, w_query, key_projection_weight, value_projection_weight, documents):
    group_width = QUERY_HEADS // KEY_VALUE_HEADS
    score_scale = 1.0 / math.sqrt(HEAD_SIZE)
    windows = tokens.reshape(N_ROWS, WINDOW_TOKENS, MODEL_WIDTH)

    def one_window(inputs):
        window, doc_ids = inputs
        normalized_input = rms_normed(window, norm_gain)
        positions = jnp.arange(WINDOW_TOKENS, dtype=jnp.int32)
        query_proj = jnp.dot(normalized_input, w_query, preferred_element_type=jnp.float32).reshape(WINDOW_TOKENS, QUERY_HEADS, HEAD_SIZE)
        key_projected = jnp.dot(normalized_input, key_projection_weight, preferred_element_type=jnp.float32).reshape(WINDOW_TOKENS, KEY_VALUE_HEADS, HEAD_SIZE)
        query_vectors_all = rotary(query_proj, positions).astype(jnp.bfloat16)
        keys_all = rotary(key_projected, positions).astype(jnp.bfloat16)
        value_vectors_all = jnp.dot(normalized_input, value_projection_weight, preferred_element_type=jnp.float32).astype(jnp.bfloat16).reshape(WINDOW_TOKENS, KEY_VALUE_HEADS, HEAD_SIZE)
        visible = (doc_ids[:, None] == doc_ids[None, :]) & (positions[:, None] >= positions[None, :])
        grouped_heads = query_vectors_all.reshape(WINDOW_TOKENS, KEY_VALUE_HEADS, group_width, HEAD_SIZE)

        def single_head(head_index):
            query_head = lax.dynamic_index_in_dim(grouped_heads, head_index, 1, keepdims=False)
            key_head = lax.dynamic_index_in_dim(keys_all, head_index, 1, keepdims=False)
            value_head = lax.dynamic_index_in_dim(value_vectors_all, head_index, 1, keepdims=False)
            scores = jnp.einsum('pgd,jd->gpj', query_head.astype(jnp.float32), key_head.astype(jnp.float32)) * score_scale
            scores = jnp.where(visible[None], scores, -1e+30)
            row_max = lax.optimization_barrier(jnp.max(scores, axis=-1, keepdims=True))
            weights = jnp.where(visible[None], jnp.exp(scores - row_max), 0.0)
            row_total = lax.optimization_barrier(jnp.sum(weights, axis=-1))
            rounded = weights.astype(jnp.bfloat16)
            mixed_out = jnp.einsum('gpj,jd->gpd', rounded.astype(jnp.float32), value_head.astype(jnp.float32))
            return mixed_out / row_total[..., None]
        split_by_head = lax.map(single_head, jnp.arange(KEY_VALUE_HEADS, dtype=jnp.int32))
        return jnp.transpose(split_by_head, (2, 0, 1, 3)).reshape(WINDOW_TOKENS, QUERY_HEADS * HEAD_SIZE).astype(jnp.bfloat16)
    outputs = lax.map(one_window, (windows, documents))
    return outputs.reshape(N_ROWS * WINDOW_TOKENS, QUERY_HEADS * HEAD_SIZE)
```

```python
import functools
import math

import jax
import jax.numpy as jnp
import numpy as np
from jax import lax
from jax.experimental import pallas as pl
from jax.experimental.pallas import tpu as pltpu
from jax.sharding import PartitionSpec as P

HEAD = 128
MOST = 1024
TQ = 128
BF16 = jnp.bfloat16
F32 = jnp.float32
MESH = pl.DeviceIdType.MESH


def rotary_table(window):
    half = HEAD // 2
    frequency = np.exp(
        np.arange(half, dtype=np.float32) * np.float32(-2.0 * math.log(500000.0) / HEAD)
    ).astype(np.float32)
    angles = np.arange(window, dtype=np.float32)[:, None] * frequency[None, :]
    return np.concatenate([np.cos(angles), np.sin(angles)], axis=1).astype(np.float32)


def kernel(
    n_rows, n_attn, back, chunk,
    tok, gain, wq, wk, wv, docs, table, out,
    xt, xn, wkv_buf, wq_buf, kv, q, tab, kdoc, qdoc,
    tok_sem, own_sem, w_send, w_recv, kv_send, kv_recv,
):
    rows = tok.shape[0]
    depth = wk.shape[0]
    kvw = wk.shape[1]
    qw = wq.shape[1]
    kv_heads = kvw // HEAD
    group = qw // kvw
    chunks = rows // chunk
    tiles = rows // TQ
    mine = back * rows
    span = min(mine + rows, -(-(MOST - 1 + TQ) // TQ) * TQ)
    me = lax.axis_index("rows")
    at = lax.axis_index("attn")

    tok_copies = [
        pltpu.make_async_copy(
            tok.at[pl.ds(c * chunk, chunk)], xt.at[pl.ds(c * chunk, chunk)], tok_sem.at[c]
        )
        for c in range(chunks)
    ]
    own_copies = [
        pltpu.make_async_copy(wk, wkv_buf.at[0, :, pl.ds(0, kvw)], own_sem.at[0]),
        pltpu.make_async_copy(wv, wkv_buf.at[0, :, pl.ds(kvw, kvw)], own_sem.at[1]),
        pltpu.make_async_copy(wq, wq_buf.at[0], own_sem.at[2]),
        pltpu.make_async_copy(
            table.at[pl.ds(pl.multiple_of(at * rows, rows), rows)], tab, own_sem.at[3]
        ),
    ]
    tok_copies[0].start()
    own_copies[0].start()
    own_copies[1].start()
    for copy in tok_copies[1:]:
        copy.start()
    own_copies[3].start()
    own_copies[2].start()

    barrier = pltpu.get_barrier_semaphore()
    for d in range(1, n_rows):
        pl.semaphore_signal(
            barrier, inc=1, device_id={"rows": lax.rem(me + d, n_rows)}, device_id_type=MESH
        )
    has_prev = at > 0
    has_next = at < n_attn - 1
    if back:

        @pl.when(has_prev)
        def _():
            pl.semaphore_signal(
                barrier, inc=1, device_id={"attn": at - 1}, device_id_type=MESH
            )

        @pl.when(has_next)
        def _():
            pl.semaphore_signal(
                barrier, inc=1, device_id={"attn": at + 1}, device_id_type=MESH
            )

        pl.semaphore_wait(
            barrier, n_rows - 1 + has_prev.astype(jnp.int32) + has_next.astype(jnp.int32)
        )
    elif n_rows > 1:
        pl.semaphore_wait(barrier, n_rows - 1)

    def weight_copy(d, which):
        src, dst = (
            (wk, wkv_buf.at[d, :, pl.ds(0, kvw)]),
            (wv, wkv_buf.at[d, :, pl.ds(kvw, kvw)]),
            (wq, wq_buf.at[d]),
        )[which]
        return pltpu.make_async_remote_copy(
            src_ref=src, dst_ref=dst,
            send_sem=w_send.at[d, which], recv_sem=w_recv.at[d, which],
            device_id={"rows": lax.rem(me + d, n_rows)}, device_id_type=MESH,
        )

    for which in range(3):
        for d in range(1, n_rows):
            weight_copy(d, which).start()

    for s in range(back + 1):
        block = at - back + s
        keep = pl.multiple_of(jnp.maximum(block, 0) * rows, rows)
        kdoc[:, pl.ds(s * rows, rows)] = jnp.where(block >= 0, docs[:, pl.ds(keep, rows)], -1)
    for t in range(tiles):
        row = kdoc[:, pl.ds(mine + t * TQ, TQ)]
        qdoc[pl.ds(t * TQ, TQ), :] = jnp.broadcast_to(row, (TQ, TQ)).T
    for s in range(back):

        @pl.when(at - back + s < 0)
        def _():
            kv[pl.ds(s * rows, rows), :] = jnp.zeros((rows, 2 * kvw), BF16)

    lane = lax.broadcasted_iota(jnp.int32, (1, HEAD), 1)

    def tables(start, size):
        t = tab[pl.ds(start, size), :]
        swapped = pltpu.roll(t, HEAD // 2, 1)
        low = lane < HEAD // 2
        return jnp.where(low, t, swapped), jnp.where(low, -swapped, t)

    def rotate(u, cosine, sine):
        return (u * cosine + pltpu.roll(u, HEAD // 2, 1) * sine).astype(BF16)

    def project(start, size, weights):
        total = None
        for d in range(n_rows):
            owner = lax.rem(me - d + n_rows, n_rows)
            part = jnp.dot(
                xn[pl.ds(start, size), pl.ds(pl.multiple_of(owner * depth, depth), depth)],
                weights[d],
                preferred_element_type=F32,
            )
            total = part if total is None else total + part
        return total

    def hop(s, c):
        return pltpu.make_async_remote_copy(
            src_ref=kv.at[pl.ds((back - s) * rows + c * chunk, chunk)],
            dst_ref=kv.at[pl.ds((back - s - 1) * rows + c * chunk, chunk)],
            send_sem=kv_send.at[s, c], recv_sem=kv_recv.at[s, c],
            device_id={"attn": jnp.minimum(at + 1, n_attn - 1)}, device_id_type=MESH,
        )

    strip = 16
    for c in range(chunks):
        tok_copies[c].wait()

        @pl.loop(0, chunk // strip)
        def _(i):
            here = pl.ds(pl.multiple_of(c * chunk + i * strip, strip), strip)
            x = xt[here, :].astype(F32)
            scale = lax.rsqrt(jnp.mean(x * x, axis=-1, keepdims=True) + 1e-05)
            xn[here, :] = (x * scale * gain[...].astype(F32)).astype(BF16)

        if c == 0:
            own_copies[0].wait()
            own_copies[1].wait()
            own_copies[3].wait()
            for d in range(1, n_rows):
                weight_copy(d, 0).wait()
                weight_copy(d, 1).wait()
        total = project(c * chunk, chunk, wkv_buf)
        cosine, sine = tables(c * chunk, chunk)
        here = pl.ds(mine + c * chunk, chunk)
        for h in range(kv_heads):
            kv[here, pl.ds(h * HEAD, HEAD)] = rotate(
                total[:, h * HEAD : (h + 1) * HEAD], cosine, sine
            )
        kv[here, pl.ds(kvw, kvw)] = total[:, kvw:].astype(BF16)
        if back:

            @pl.when(has_next)
            def _():
                hop(0, c).start()

    own_copies[2].wait()
    for d in range(1, n_rows):
        weight_copy(d, 2).wait()
    for c in range(chunks):
        total = project(c * chunk, chunk, wq_buf)
        cosine, sine = tables(c * chunk, chunk)
        for h in range(kv_heads):
            for g in range(group):
                col = (h * group + g) * HEAD
                u = rotate(total[:, col : col + HEAD], cosine, sine)
                for t in range(chunk // TQ):
                    q[c * (chunk // TQ) + t, h, pl.ds(g * TQ, TQ), :] = u[
                        t * TQ : (t + 1) * TQ
                    ]

    for s in range(back):
        for c in range(chunks):

            @pl.when(at > s)
            def _():
                hop(s, c).wait_recv()

            if s + 1 < back:

                @pl.when((at > s) & has_next)
                def _():
                    hop(s + 1, c).start()

    factor = math.log2(math.e) / math.sqrt(HEAD)

    @pl.loop(0, tiles)
    def _(t):
        first = pl.multiple_of(t * TQ, TQ)
        begin = pl.multiple_of(jnp.maximum(mine + first + TQ - span, 0), TQ)
        query_at = lax.broadcasted_iota(jnp.int32, (TQ, 1), 0) + (mine + first)
        key_at = lax.broadcasted_iota(jnp.int32, (1, span), 1) + begin
        visible = (qdoc[pl.ds(first, TQ), :][:, :1] == kdoc[:, pl.ds(begin, span)]) & (
            query_at >= key_at
        )
        for h in range(kv_heads):
            keys = kv[pl.ds(begin, span), pl.ds(h * HEAD, HEAD)]
            vals = kv[pl.ds(begin, span), pl.ds(kvw + h * HEAD, HEAD)]
            for g in range(group):
                s = lax.dot_general(
                    q[t, h, pl.ds(g * TQ, TQ), :], keys, (((1,), (1,)), ((), ())),
                    preferred_element_type=F32,
                )
                s = jnp.where(visible, s, -1e30)
                p = jnp.exp2((s - jnp.max(s, axis=-1, keepdims=True)) * factor)
                total = jnp.sum(p, axis=-1, keepdims=True)
                mixed = jnp.dot(p.astype(BF16), vals, preferred_element_type=F32)
                out[pl.ds(first, TQ), pl.ds((h * group + g) * HEAD, HEAD)] = (
                    mixed / total
                ).astype(BF16)

    for s in range(back):
        for c in range(chunks):

            @pl.when((at >= s) & has_next)
            def _():
                hop(s, c).wait_send()


def solution(mesh):
    n_rows = mesh.shape["rows"]
    n_attn = mesh.shape["attn"]

    def on_device(tokens, norm_gain, w_query, w_key, w_value, documents):
        rows, width = tokens.shape
        depth, qw = w_query.shape
        kvw = w_key.shape[1]
        back = min(n_attn - 1, -(-(MOST - 1) // rows))
        chunk = min(rows, 256)
        chunks = rows // chunk
        table = jnp.asarray(rotary_table(documents.shape[1]))
        anywhere = pl.BlockSpec(memory_space=pl.ANY)
        vmem = pl.BlockSpec(memory_space=pltpu.VMEM)
        keys = (back + 1) * rows
        group = qw // kvw
        return pl.pallas_call(
            functools.partial(kernel, n_rows, n_attn, back, chunk),
            out_shape=jax.ShapeDtypeStruct((rows, qw), BF16),
            in_specs=[anywhere, vmem, anywhere, anywhere, anywhere, vmem, anywhere],
            out_specs=vmem,
            scratch_shapes=[
                pltpu.VMEM((rows, width), BF16),
                pltpu.VMEM((rows, width), BF16),
                pltpu.VMEM((n_rows, depth, 2 * kvw), BF16),
                pltpu.VMEM((n_rows, depth, qw), BF16),
                pltpu.VMEM((keys, 2 * kvw), BF16),
                pltpu.VMEM((rows // TQ, kvw // HEAD, group * TQ, HEAD), BF16),
                pltpu.VMEM((rows, HEAD), F32),
                pltpu.VMEM((1, keys), jnp.int32),
                pltpu.VMEM((rows, TQ), jnp.int32),
                pltpu.SemaphoreType.DMA((chunks,)),
                pltpu.SemaphoreType.DMA((4,)),
                pltpu.SemaphoreType.DMA((n_rows, 3)),
                pltpu.SemaphoreType.DMA((n_rows, 3)),
                pltpu.SemaphoreType.DMA((max(back, 1), chunks)),
                pltpu.SemaphoreType.DMA((max(back, 1), chunks)),
            ],
            compiler_params=pltpu.CompilerParams(
                collective_id=0, has_side_effects=True, vmem_limit_bytes=60 << 20
            ),
            name="layer",
        )(tokens, norm_gain.reshape(1, width), w_query, w_key, w_value, documents, table)

    placed = (
        P(("rows", "attn"), None),
        P(),
        P("rows", "tp"),
        P("rows", "tp"),
        P("rows", "tp"),
        P("rows", None),
    )
    return jax.shard_map(
        on_device, mesh=mesh, in_specs=placed, out_specs=P(("rows", "attn"), "tp"), check_vma=False
    )
```

```python
import functools
import math

import jax
import jax.numpy as jnp
import numpy as np
from jax import lax
from jax.experimental import pallas as pl
from jax.experimental.pallas import tpu as pltpu
from jax.sharding import PartitionSpec as P

HEAD = 128
MOST = 1024
TQ = 128
BF16 = jnp.bfloat16
F32 = jnp.float32
MESH = pl.DeviceIdType.MESH


def rotary_table(window):
    half = HEAD // 2
    frequency = np.exp(
        np.arange(half, dtype=np.float32) * np.float32(-2.0 * math.log(500000.0) / HEAD)
    ).astype(np.float32)
    angles = np.arange(window, dtype=np.float32)[:, None] * frequency[None, :]
    return np.concatenate([np.cos(angles), np.sin(angles)], axis=1).astype(np.float32)


def kernel(
    n_rows, n_attn, back, chunk,
    tok, gain, wq, wk, wv, docs, table, out,
    xt, xn, wkv_buf, wq_buf, kv, q, tab, kdoc, qdoc,
    tok_sem, own_sem, w_send, w_recv, kv_send, kv_recv,
):
    rows = tok.shape[0]
    depth = wk.shape[0]
    kvw = wk.shape[1]
    qw = wq.shape[1]
    kv_heads = kvw // HEAD
    group = qw // kvw
    chunks = rows // chunk
    tiles = rows // TQ
    mine = back * rows
    span = min(mine + rows, -(-(MOST - 1 + TQ) // TQ) * TQ)
    me = lax.axis_index("rows")
    at = lax.axis_index("attn")

    tok_copies = [
        pltpu.make_async_copy(
            tok.at[pl.ds(c * chunk, chunk)], xt.at[pl.ds(c * chunk, chunk)], tok_sem.at[c]
        )
        for c in range(chunks)
    ]
    own_copies = [
        pltpu.make_async_copy(wk, wkv_buf.at[0, :, pl.ds(0, kvw)], own_sem.at[0]),
        pltpu.make_async_copy(wv, wkv_buf.at[0, :, pl.ds(kvw, kvw)], own_sem.at[1]),
        pltpu.make_async_copy(wq, wq_buf.at[0], own_sem.at[2]),
        pltpu.make_async_copy(
            table.at[pl.ds(pl.multiple_of(at * rows, rows), rows)], tab, own_sem.at[3]
        ),
    ]
    tok_copies[-1].start()
    own_copies[0].start()
    own_copies[1].start()
    own_copies[3].start()
    for copy in tok_copies[-2::-1]:
        copy.start()

    barrier = pltpu.get_barrier_semaphore()
    for d in range(1, n_rows):
        pl.semaphore_signal(
            barrier, inc=1, device_id={"rows": lax.rem(me + d, n_rows)}, device_id_type=MESH
        )
    has_prev = at > 0
    has_next = at < n_attn - 1
    if back:

        @pl.when(has_prev)
        def _():
            pl.semaphore_signal(
                barrier, inc=1, device_id={"attn": at - 1}, device_id_type=MESH
            )

        @pl.when(has_next)
        def _():
            pl.semaphore_signal(
                barrier, inc=1, device_id={"attn": at + 1}, device_id_type=MESH
            )

        pl.semaphore_wait(
            barrier, n_rows - 1 + has_prev.astype(jnp.int32) + has_next.astype(jnp.int32)
        )
    elif n_rows > 1:
        pl.semaphore_wait(barrier, n_rows - 1)

    def weight_copy(d, which):
        src, dst = (
            (wk, wkv_buf.at[d, :, pl.ds(0, kvw)]),
            (wv, wkv_buf.at[d, :, pl.ds(kvw, kvw)]),
            (wq, wq_buf.at[d]),
        )[which]
        return pltpu.make_async_remote_copy(
            src_ref=src, dst_ref=dst,
            send_sem=w_send.at[d, which], recv_sem=w_recv.at[d, which],
            device_id={"rows": lax.rem(me + d, n_rows)}, device_id_type=MESH,
        )

    for which in range(3):
        for d in range(1, n_rows):
            weight_copy(d, which).start()
    own_copies[2].start()

    for s in range(back + 1):
        block = at - back + s
        keep = pl.multiple_of(jnp.maximum(block, 0) * rows, rows)
        kdoc[:, pl.ds(s * rows, rows)] = jnp.where(block >= 0, docs[:, pl.ds(keep, rows)], -1)
    for t in range(tiles):
        row = kdoc[:, pl.ds(mine + t * TQ, TQ)]
        qdoc[pl.ds(t * TQ, TQ), :] = jnp.broadcast_to(row, (TQ, TQ)).T
    for s in range(back):

        @pl.when(at - back + s < 0)
        def _():
            kv[pl.ds(s * rows, rows), :] = jnp.zeros((rows, 2 * kvw), BF16)

    lane = lax.broadcasted_iota(jnp.int32, (1, HEAD), 1)

    def tables(start, size):
        t = tab[pl.ds(start, size), :]
        swapped = pltpu.roll(t, HEAD // 2, 1)
        low = lane < HEAD // 2
        return jnp.where(low, t, swapped), jnp.where(low, -swapped, t)

    def rotate(u, cosine, sine):
        return (u * cosine + pltpu.roll(u, HEAD // 2, 1) * sine).astype(BF16)

    def project(start, size, weights):
        total = None
        for d in range(n_rows):
            owner = lax.rem(me - d + n_rows, n_rows)
            part = jnp.dot(
                xn[pl.ds(start, size), pl.ds(pl.multiple_of(owner * depth, depth), depth)],
                weights[d],
                preferred_element_type=F32,
            )
            total = part if total is None else total + part
        return total

    def hop(s, c):
        return pltpu.make_async_remote_copy(
            src_ref=kv.at[pl.ds((back - s) * rows + c * chunk, chunk)],
            dst_ref=kv.at[pl.ds((back - s - 1) * rows + c * chunk, chunk)],
            send_sem=kv_send.at[s, c], recv_sem=kv_recv.at[s, c],
            device_id={"attn": jnp.minimum(at + 1, n_attn - 1)}, device_id_type=MESH,
        )

    def arrived(s, c):
        @pl.when(at > s)
        def _():
            hop(s, c).wait_recv()

        if s + 1 < back:

            @pl.when((at > s) & has_next)
            def _():
                hop(s + 1, c).start()

    strip = 16
    for c in reversed(range(chunks)):
        tok_copies[c].wait()

        @pl.loop(0, chunk // strip, unroll=2)
        def _(i):
            here = pl.ds(pl.multiple_of(c * chunk + i * strip, strip), strip)
            x = xt[here, :].astype(F32)
            scale = lax.rsqrt(jnp.mean(x * x, axis=-1, keepdims=True) + 1e-05)
            xn[here, :] = (x * scale * gain[...].astype(F32).reshape(1, -1)).astype(BF16)

        if c == chunks - 1:
            own_copies[0].wait()
            own_copies[1].wait()
            own_copies[3].wait()
            for d in range(1, n_rows):
                weight_copy(d, 0).wait()
                weight_copy(d, 1).wait()
        total = project(c * chunk, chunk, wkv_buf)
        cosine, sine = tables(c * chunk, chunk)
        here = pl.ds(mine + c * chunk, chunk)
        for h in range(kv_heads):
            kv[here, pl.ds(h * HEAD, HEAD)] = rotate(
                total[:, h * HEAD : (h + 1) * HEAD], cosine, sine
            )
        kv[here, pl.ds(kvw, kvw)] = total[:, kvw:].astype(BF16)
        if back:

            @pl.when(has_next)
            def _():
                hop(0, c).start()

    relayed = [(s, c) for s in range(back - 1) for c in reversed(range(chunks))]
    last = [(back - 1, c) for c in reversed(range(chunks))] if back else []

    own_copies[2].wait()
    for d in range(1, n_rows):
        weight_copy(d, 2).wait()
    part = min(rows, 2 * chunk)
    for step in reversed(range(rows // part)):
        for _ in range(min(1, len(relayed))):
            arrived(*relayed.pop(0))
        total = project(step * part, part, wq_buf)
        cosine, sine = tables(step * part, part)
        for h in range(kv_heads):
            for g in range(group):
                col = (h * group + g) * HEAD
                u = rotate(total[:, col : col + HEAD], cosine, sine)
                for t in range(part // TQ):
                    q[step * (part // TQ) + t, h, pl.ds(g * TQ, TQ), :] = u[
                        t * TQ : (t + 1) * TQ
                    ]
    for event in relayed:
        arrived(*event)

    factor = math.log2(math.e) / math.sqrt(HEAD)

    for t in reversed(range(tiles)):
        first = t * TQ
        begin = max(mine + first + TQ - span, 0)
        while last and (last[0][1] + 1) * chunk > begin:
            arrived(*last.pop(0))
        query_at = lax.broadcasted_iota(jnp.int32, (TQ, 1), 0) + (mine + first)
        key_at = lax.broadcasted_iota(jnp.int32, (1, span), 1) + begin
        visible = (qdoc[pl.ds(first, TQ), :][:, :1] == kdoc[:, pl.ds(begin, span)]) & (
            query_at >= key_at
        )
        for h in range(kv_heads):
            keys = kv[pl.ds(begin, span), pl.ds(h * HEAD, HEAD)]
            vals = kv[pl.ds(begin, span), pl.ds(kvw + h * HEAD, HEAD)]
            s = lax.dot_general(
                q[t, h], keys, (((1,), (1,)), ((), ())), preferred_element_type=F32
            )
            s = jnp.where(visible[None], s.reshape(group, TQ, span), -1e30)
            p = jnp.exp2((s - jnp.max(s, axis=-1, keepdims=True)) * factor)
            total = jnp.sum(p, axis=-1, keepdims=True)
            mixed = jnp.dot(
                p.astype(BF16).reshape(group * TQ, span), vals, preferred_element_type=F32
            )
            mixed = (mixed.reshape(group, TQ, HEAD) / total).astype(BF16)
            for g in range(group):
                out[pl.ds(first, TQ), pl.ds((h * group + g) * HEAD, HEAD)] = mixed[g]
    for event in last:
        arrived(*event)

    for s in range(back):
        for c in range(chunks):

            @pl.when((at >= s) & has_next)
            def _():
                hop(s, c).wait_send()


def solution(mesh):
    n_rows = mesh.shape["rows"]
    n_attn = mesh.shape["attn"]

    def on_device(tokens, norm_gain, w_query, w_key, w_value, documents):
        rows, width = tokens.shape
        depth, qw = w_query.shape
        kvw = w_key.shape[1]
        back = min(n_attn - 1, -(-(MOST - 1) // rows))
        chunk = min(rows, TQ)
        chunks = rows // chunk
        table = jnp.asarray(rotary_table(documents.shape[1]))
        anywhere = pl.BlockSpec(memory_space=pl.ANY)
        vmem = pl.BlockSpec(memory_space=pltpu.VMEM)
        keys = (back + 1) * rows
        group = qw // kvw
        return pl.pallas_call(
            functools.partial(kernel, n_rows, n_attn, back, chunk),
            out_shape=jax.ShapeDtypeStruct((rows, qw), BF16),
            in_specs=[anywhere, vmem, anywhere, anywhere, anywhere, vmem, anywhere],
            out_specs=vmem,
            scratch_shapes=[
                pltpu.VMEM((rows, width), BF16),
                pltpu.VMEM((rows, width), BF16),
                pltpu.VMEM((n_rows, depth, 2 * kvw), BF16),
                pltpu.VMEM((n_rows, depth, qw), BF16),
                pltpu.VMEM((keys, 2 * kvw), BF16),
                pltpu.VMEM((rows // TQ, kvw // HEAD, group * TQ, HEAD), BF16),
                pltpu.VMEM((rows, HEAD), F32),
                pltpu.VMEM((1, keys), jnp.int32),
                pltpu.VMEM((rows, TQ), jnp.int32),
                pltpu.SemaphoreType.DMA((chunks,)),
                pltpu.SemaphoreType.DMA((4,)),
                pltpu.SemaphoreType.DMA((n_rows, 3)),
                pltpu.SemaphoreType.DMA((n_rows, 3)),
                pltpu.SemaphoreType.DMA((max(back, 1), chunks)),
                pltpu.SemaphoreType.DMA((max(back, 1), chunks)),
            ],
            compiler_params=pltpu.CompilerParams(
                collective_id=0, has_side_effects=True, vmem_limit_bytes=60 << 20
            ),
            name="layer",
        )(tokens, norm_gain, w_query, w_key, w_value, documents, table)

    placed = (
        P(("rows", "attn"), None),
        P(),
        P("rows", "tp"),
        P("rows", "tp"),
        P("rows", "tp"),
        P("rows", None),
    )
    return jax.shard_map(
        on_device, mesh=mesh, in_specs=placed, out_specs=P(("rows", "attn"), "tp"), check_vma=False
    )
```

```python
import functools
import math

import jax
import jax.numpy as jnp
import numpy as np
from jax import lax
from jax.experimental import pallas as pl
from jax.experimental.pallas import tpu as pltpu
from jax.sharding import PartitionSpec as P

HEAD = 128
MOST = 1024
TQ = 128
BF16 = jnp.bfloat16
F32 = jnp.float32
MESH = pl.DeviceIdType.MESH


def rotary_table(window):
    half = HEAD // 2
    frequency = np.exp(
        np.arange(half, dtype=np.float32) * np.float32(-2.0 * math.log(500000.0) / HEAD)
    ).astype(np.float32)
    angles = np.arange(window, dtype=np.float32)[:, None] * frequency[None, :]
    return np.concatenate([np.cos(angles), np.sin(angles)], axis=1).astype(np.float32)


def kernel(
    n_rows, n_attn, back, chunk, span,
    tok, gain, wq, wk, wv, docs, table, out,
    probs, gains, xt, xn, wkv_buf, wq_buf, kv, q, tab, kdoc, qdoc,
    tok_sem, own_sem, w_send, w_recv, kv_send, kv_recv,
):
    rows = tok.shape[0]
    depth = wk.shape[0]
    kvw = wk.shape[1]
    qw = wq.shape[1]
    kv_heads = kvw // HEAD
    group = qw // kvw
    chunks = rows // chunk
    tiles = rows // TQ
    mine = back * rows
    me = lax.axis_index("rows")
    at = lax.axis_index("attn")

    tok_copies = [
        pltpu.make_async_copy(
            tok.at[pl.ds(c * chunk, chunk)], xt.at[pl.ds(c * chunk, chunk)], tok_sem.at[c]
        )
        for c in range(chunks)
    ]
    own_copies = [
        pltpu.make_async_copy(wk, wkv_buf.at[0, :, pl.ds(0, kvw)], own_sem.at[0]),
        pltpu.make_async_copy(wv, wkv_buf.at[0, :, pl.ds(kvw, kvw)], own_sem.at[1]),
        pltpu.make_async_copy(wq, wq_buf.at[0], own_sem.at[2]),
        pltpu.make_async_copy(
            table.at[pl.ds(pl.multiple_of(at * rows, rows), rows)], tab, own_sem.at[3]
        ),
    ]
    tok_copies[-1].start()
    own_copies[0].start()
    own_copies[1].start()
    own_copies[3].start()
    for copy in tok_copies[-2::-1]:
        copy.start()

    barrier = pltpu.get_barrier_semaphore()
    for d in range(1, n_rows):
        pl.semaphore_signal(
            barrier, inc=1, device_id={"rows": lax.rem(me + d, n_rows)}, device_id_type=MESH
        )
    has_prev = at > 0
    has_next = at < n_attn - 1
    if back:

        @pl.when(has_prev)
        def _():
            pl.semaphore_signal(
                barrier, inc=1, device_id={"attn": at - 1}, device_id_type=MESH
            )

        @pl.when(has_next)
        def _():
            pl.semaphore_signal(
                barrier, inc=1, device_id={"attn": at + 1}, device_id_type=MESH
            )

        pl.semaphore_wait(
            barrier, n_rows - 1 + has_prev.astype(jnp.int32) + has_next.astype(jnp.int32)
        )
    elif n_rows > 1:
        pl.semaphore_wait(barrier, n_rows - 1)

    cuts = 1
    cut = depth // cuts

    def weight_copies(d, which):
        src, dst = (
            (wk, wkv_buf.at[d, :, pl.ds(0, kvw)]),
            (wv, wkv_buf.at[d, :, pl.ds(kvw, kvw)]),
            (wq, wq_buf.at[d]),
        )[which]
        return [
            pltpu.make_async_remote_copy(
                src_ref=src.at[pl.ds(k * cut, cut)], dst_ref=dst.at[pl.ds(k * cut, cut)],
                send_sem=w_send.at[d, which, k], recv_sem=w_recv.at[d, which, k],
                device_id={"rows": lax.rem(me + d, n_rows)}, device_id_type=MESH,
            )
            for k in range(cuts)
        ]

    def start_weights(d, which):
        for copy in weight_copies(d, which):
            copy.start()

    def wait_weights(d, which):
        for copy in weight_copies(d, which):
            copy.wait()

    for which in range(3):
        for d in range(1, n_rows):
            start_weights(d, which)

    for s in range(back + 1):
        block = at - back + s
        keep = pl.multiple_of(jnp.maximum(block, 0) * rows, rows)
        kdoc[:, pl.ds(s * rows, rows)] = jnp.where(block >= 0, docs[:, pl.ds(keep, rows)], -1)
    for t in range(tiles):
        row = kdoc[:, pl.ds(mine + t * TQ, TQ)]
        qdoc[pl.ds(t * TQ, TQ), :] = jnp.broadcast_to(row, (TQ, TQ)).T
    for s in range(back):

        @pl.when(at - back + s < 0)
        def _():
            kv[pl.ds(s * rows, rows), :] = jnp.zeros((rows, 2 * kvw), BF16)

    lane = lax.broadcasted_iota(jnp.int32, (1, HEAD), 1)

    def tables(start, size):
        t = tab[pl.ds(start, size), :]
        swapped = pltpu.roll(t, HEAD // 2, 1)
        low = lane < HEAD // 2
        return jnp.where(low, t, swapped), jnp.where(low, -swapped, t)

    def rotate(u, cosine, sine):
        return (u * cosine + pltpu.roll(u, HEAD // 2, 1) * sine).astype(BF16)

    def project(start, size, weights):
        total = None
        for d in range(n_rows):
            owner = lax.rem(me - d + n_rows, n_rows)
            part = jnp.dot(
                xn[pl.ds(start, size), pl.ds(pl.multiple_of(owner * depth, depth), depth)],
                weights(d),
                preferred_element_type=F32,
            )
            total = part if total is None else total + part
        return total

    def hop(s, c):
        return pltpu.make_async_remote_copy(
            src_ref=kv.at[pl.ds((back - s) * rows + c * chunk, chunk)],
            dst_ref=kv.at[pl.ds((back - s - 1) * rows + c * chunk, chunk)],
            send_sem=kv_send.at[s, c], recv_sem=kv_recv.at[s, c],
            device_id={"attn": jnp.minimum(at + 1, n_attn - 1)}, device_id_type=MESH,
        )

    def arrived(s, c):
        @pl.when(at > s)
        def _():
            hop(s, c).wait_recv()

        if s + 1 < back:

            @pl.when((at > s) & has_next)
            def _():
                hop(s + 1, c).start()

    half = min(rows, 2 * chunk)
    q_rows = rows
    strip, piece = 16, 256
    width = tok.shape[1]
    gains[...] = jnp.broadcast_to(gain[...].astype(F32).reshape(1, -1), gains.shape)
    for c in reversed(range(chunks)):
        tok_copies[c].wait()

        @pl.loop(0, chunk // strip, unroll=4)
        def _(i):
            here = pl.ds(pl.multiple_of(c * chunk + i * strip, strip), strip)
            squares = jnp.zeros((strip, piece), F32)
            for k in range(width // piece):
                x = xt[here, pl.ds(k * piece, piece)].astype(F32)
                squares = squares + x * x
            mean_sq = jnp.sum(squares, axis=-1, keepdims=True) * (1.0 / width)
            scale = jnp.broadcast_to(lax.rsqrt(mean_sq + 1e-05), (strip, piece))
            for k in range(width // piece):
                cols = pl.ds(k * piece, piece)
                x = xt[here, cols].astype(F32) * scale
                xn[here, cols] = (
                    x.reshape(strip // 8, 8, piece) * gains[:, cols][None]
                ).reshape(strip, piece).astype(BF16)

        if c == chunks - 1:
            own_copies[0].wait()
            own_copies[1].wait()
            own_copies[3].wait()
            for d in range(1, n_rows):
                wait_weights(d, 0)
                wait_weights(d, 1)
            own_copies[2].start()
        if c % (half // chunk):
            continue
        total = project(c * chunk, half, lambda d: wkv_buf[d])
        cosine, sine = tables(c * chunk, half)
        here = pl.ds(mine + c * chunk, half)
        for h in range(kv_heads):
            kv[here, pl.ds(h * HEAD, HEAD)] = rotate(
                total[:, h * HEAD : (h + 1) * HEAD], cosine, sine
            )
        kv[here, pl.ds(kvw, kvw)] = total[:, kvw:].astype(BF16)
        if back:

            @pl.when(has_next)
            def _():
                for k in reversed(range(half // chunk)):
                    hop(0, c + k).start()

    relayed = [(s, c) for s in range(back - 1) for c in reversed(range(chunks))]
    last = [(back - 1, c) for c in reversed(range(chunks))] if back else []

    own_copies[2].wait()
    for d in range(1, n_rows):
        wait_weights(d, 2)
    for step in reversed(range(rows // q_rows)):
        if relayed:
            arrived(*relayed.pop(0))
        total = project(step * q_rows, q_rows, lambda d: wq_buf[d])
        cosine, sine = tables(step * q_rows, q_rows)
        for h in range(kv_heads):
            for g in range(group):
                col = (h * group + g) * HEAD
                u = rotate(total[:, col : col + HEAD], cosine, sine)
                for t in range(q_rows // TQ):
                    q[step * (q_rows // TQ) + t, h, pl.ds(g * TQ, TQ), :] = u[
                        t * TQ : (t + 1) * TQ
                    ]
    for event in relayed:
        arrived(*event)

    factor = math.log2(math.e) / math.sqrt(HEAD)

    for t in reversed(range(tiles)):
        first = t * TQ
        begin = max(mine + first + TQ - span, 0)
        while last and (last[0][1] + 1) * chunk > begin:
            arrived(*last.pop(0))
        query_at = lax.broadcasted_iota(jnp.int32, (TQ, 1), 0) + (mine + first)
        key_at = lax.broadcasted_iota(jnp.int32, (1, span), 1) + begin
        visible = (qdoc[pl.ds(first, TQ), :][:, :1] == kdoc[:, pl.ds(begin, span)]) & (
            query_at >= key_at
        )
        for h in range(kv_heads):
            keys = kv[pl.ds(begin, span), pl.ds(h * HEAD, HEAD)]
            vals = kv[pl.ds(begin, span), pl.ds(kvw + h * HEAD, HEAD)]
            s = lax.dot_general(
                q[t, h], keys, (((1,), (1,)), ((), ())), preferred_element_type=F32
            )
            totals = []
            for r in range(0, group * TQ, strip):
                seen = visible[r % TQ : r % TQ + strip]
                part = jnp.where(seen, s[r : r + strip], -1e30)
                p = jnp.exp2((part - jnp.max(part, axis=-1, keepdims=True)) * factor)
                totals.append(jnp.sum(p, axis=-1, keepdims=True))
                probs[pl.ds(r, strip), :] = p.astype(BF16)
            total = jnp.concatenate(totals, axis=0).reshape(group, TQ, 1)
            mixed = jnp.dot(probs[...], vals, preferred_element_type=F32)
            mixed = (mixed.reshape(group, TQ, HEAD) / total).astype(BF16)
            for g in range(group):
                out[pl.ds(first, TQ), pl.ds((h * group + g) * HEAD, HEAD)] = mixed[g]
    for event in last:
        arrived(*event)

    for s in range(back):
        for c in range(chunks):

            @pl.when((at >= s) & has_next)
            def _():
                hop(s, c).wait_send()


def solution(mesh):
    n_rows = mesh.shape["rows"]
    n_attn = mesh.shape["attn"]

    def on_device(tokens, norm_gain, w_query, w_key, w_value, documents):
        rows, width = tokens.shape
        depth, qw = w_query.shape
        kvw = w_key.shape[1]
        back = min(n_attn - 1, -(-(MOST - 1) // rows))
        chunk = min(rows, TQ)
        chunks = rows // chunk
        table = jnp.asarray(rotary_table(documents.shape[1]))
        anywhere = pl.BlockSpec(memory_space=pl.ANY)
        vmem = pl.BlockSpec(memory_space=pltpu.VMEM)
        keys = (back + 1) * rows
        span = min(keys, -(-(MOST - 1 + TQ) // TQ) * TQ)
        group = qw // kvw
        return pl.pallas_call(
            functools.partial(kernel, n_rows, n_attn, back, chunk, span),
            out_shape=jax.ShapeDtypeStruct((rows, qw), BF16),
            in_specs=[anywhere, vmem, anywhere, anywhere, anywhere, vmem, anywhere],
            out_specs=vmem,
            scratch_shapes=[
                pltpu.VMEM((group * TQ, span), BF16),
                pltpu.VMEM((8, width), F32),
                pltpu.VMEM((rows, width), BF16),
                pltpu.VMEM((rows, width), BF16),
                pltpu.VMEM((n_rows, depth, 2 * kvw), BF16),
                pltpu.VMEM((n_rows, depth, qw), BF16),
                pltpu.VMEM((keys, 2 * kvw), BF16),
                pltpu.VMEM((rows // TQ, kvw // HEAD, group * TQ, HEAD), BF16),
                pltpu.VMEM((rows, HEAD), F32),
                pltpu.VMEM((1, keys), jnp.int32),
                pltpu.VMEM((rows, TQ), jnp.int32),
                pltpu.SemaphoreType.DMA((chunks,)),
                pltpu.SemaphoreType.DMA((4,)),
                pltpu.SemaphoreType.DMA((n_rows, 3, 4)),
                pltpu.SemaphoreType.DMA((n_rows, 3, 4)),
                pltpu.SemaphoreType.DMA((max(back, 1), chunks)),
                pltpu.SemaphoreType.DMA((max(back, 1), chunks)),
            ],
            compiler_params=pltpu.CompilerParams(
                collective_id=0, has_side_effects=True, vmem_limit_bytes=60 << 20
            ),
            name="layer",
        )(tokens, norm_gain, w_query, w_key, w_value, documents, table)

    placed = (
        P(("rows", "attn"), None),
        P(),
        P("rows", "tp"),
        P("rows", "tp"),
        P("rows", "tp"),
        P("rows", None),
    )
    return jax.shard_map(
        on_device, mesh=mesh, in_specs=placed, out_specs=P(("rows", "attn"), "tp"), check_vma=False
    )
```

```python
import functools
import math

import jax
import jax.numpy as jnp
import numpy as np
from jax import lax
from jax.experimental import pallas as pl
from jax.experimental.pallas import tpu as pltpu
from jax.sharding import PartitionSpec as P

HEAD = 128
MOST = 1024
TQ = 128
BF16 = jnp.bfloat16
F32 = jnp.float32
MESH = pl.DeviceIdType.MESH


def rotary_table(window):
    half = HEAD // 2
    frequency = np.exp(
        np.arange(half, dtype=np.float32) * np.float32(-2.0 * math.log(500000.0) / HEAD)
    ).astype(np.float32)
    angles = np.arange(window, dtype=np.float32)[:, None] * frequency[None, :]
    return np.concatenate([np.cos(angles), np.sin(angles)], axis=1).astype(np.float32)


def kernel(
    n_rows, n_attn, back, chunk,
    tok, gain, wq, wk, wv, docs, table, out,
    gains, xt, xn, wkv_buf, wq_buf, kv, q, tab, kdoc, qdoc,
    tok_sem, own_sem, w_send, w_recv, kv_send, kv_recv,
):
    rows = tok.shape[0]
    depth = wk.shape[0]
    kvw = wk.shape[1]
    qw = wq.shape[1]
    kv_heads = kvw // HEAD
    group = qw // kvw
    chunks = rows // chunk
    tiles = rows // TQ
    mine = back * rows
    span = min(mine + rows, -(-(MOST - 1 + TQ) // TQ) * TQ)
    me = lax.axis_index("rows")
    at = lax.axis_index("attn")

    tok_copies = [
        pltpu.make_async_copy(
            tok.at[pl.ds(c * chunk, chunk)], xt.at[pl.ds(c * chunk, chunk)], tok_sem.at[c]
        )
        for c in range(chunks)
    ]
    own_copies = [
        pltpu.make_async_copy(wk, wkv_buf.at[0, :, pl.ds(0, kvw)], own_sem.at[0]),
        pltpu.make_async_copy(wv, wkv_buf.at[0, :, pl.ds(kvw, kvw)], own_sem.at[1]),
        pltpu.make_async_copy(wq, wq_buf.at[0], own_sem.at[2]),
        pltpu.make_async_copy(
            table.at[pl.ds(pl.multiple_of(at * rows, rows), rows)], tab, own_sem.at[3]
        ),
    ]
    tok_copies[-1].start()
    own_copies[0].start()
    own_copies[1].start()
    own_copies[3].start()
    for copy in tok_copies[-2::-1]:
        copy.start()

    barrier = pltpu.get_barrier_semaphore()
    for d in range(1, n_rows):
        pl.semaphore_signal(
            barrier, inc=1, device_id={"rows": lax.rem(me + d, n_rows)}, device_id_type=MESH
        )
    has_prev = at > 0
    has_next = at < n_attn - 1
    if back:

        @pl.when(has_prev)
        def _():
            pl.semaphore_signal(
                barrier, inc=1, device_id={"attn": at - 1}, device_id_type=MESH
            )

        @pl.when(has_next)
        def _():
            pl.semaphore_signal(
                barrier, inc=1, device_id={"attn": at + 1}, device_id_type=MESH
            )

        pl.semaphore_wait(
            barrier, n_rows - 1 + has_prev.astype(jnp.int32) + has_next.astype(jnp.int32)
        )
    elif n_rows > 1:
        pl.semaphore_wait(barrier, n_rows - 1)

    def weight_copy(d, which):
        src, dst = (
            (wk, wkv_buf.at[d, :, pl.ds(0, kvw)]),
            (wv, wkv_buf.at[d, :, pl.ds(kvw, kvw)]),
            (wq, wq_buf.at[d]),
        )[which]
        return pltpu.make_async_remote_copy(
            src_ref=src, dst_ref=dst,
            send_sem=w_send.at[d, which], recv_sem=w_recv.at[d, which],
            device_id={"rows": lax.rem(me + d, n_rows)}, device_id_type=MESH,
        )

    for which in range(3):
        for d in range(1, n_rows):
            weight_copy(d, which).start()
    own_copies[2].start()

    for s in range(back + 1):
        block = at - back + s
        keep = pl.multiple_of(jnp.maximum(block, 0) * rows, rows)
        kdoc[:, pl.ds(s * rows, rows)] = jnp.where(block >= 0, docs[:, pl.ds(keep, rows)], -1)
    for t in range(tiles):
        row = kdoc[:, pl.ds(mine + t * TQ, TQ)]
        qdoc[pl.ds(t * TQ, TQ), :] = jnp.broadcast_to(row, (TQ, TQ)).T
    for s in range(back):

        @pl.when(at - back + s < 0)
        def _():
            kv[pl.ds(s * rows, rows), :] = jnp.zeros((rows, 2 * kvw), BF16)

    lane = lax.broadcasted_iota(jnp.int32, (1, HEAD), 1)

    def tables(start, size):
        t = tab[pl.ds(start, size), :]
        swapped = pltpu.roll(t, HEAD // 2, 1)
        low = lane < HEAD // 2
        return jnp.where(low, t, swapped), jnp.where(low, -swapped, t)

    def rotate(u, cosine, sine):
        return (u * cosine + pltpu.roll(u, HEAD // 2, 1) * sine).astype(BF16)

    def project(start, size, weights):
        total = None
        for d in range(n_rows):
            owner = lax.rem(me - d + n_rows, n_rows)
            part = jnp.dot(
                xn[pl.ds(start, size), pl.ds(pl.multiple_of(owner * depth, depth), depth)],
                weights[d],
                preferred_element_type=F32,
            )
            total = part if total is None else total + part
        return total

    def hop(s, c):
        return pltpu.make_async_remote_copy(
            src_ref=kv.at[pl.ds((back - s) * rows + c * chunk, chunk)],
            dst_ref=kv.at[pl.ds((back - s - 1) * rows + c * chunk, chunk)],
            send_sem=kv_send.at[s, c], recv_sem=kv_recv.at[s, c],
            device_id={"attn": jnp.minimum(at + 1, n_attn - 1)}, device_id_type=MESH,
        )

    def arrived(s, c):
        @pl.when(at > s)
        def _():
            hop(s, c).wait_recv()

        if s + 1 < back:

            @pl.when((at > s) & has_next)
            def _():
                hop(s + 1, c).start()

    relayed = [(s, c) for s in range(back - 1) for c in reversed(range(chunks))]
    strip, piece = 16, 256
    width = tok.shape[1]
    gains[...] = jnp.broadcast_to(gain[...].astype(F32).reshape(1, -1), gains.shape)
    for c in reversed(range(chunks)):
        if c == 0 and relayed:
            arrived(*relayed.pop(0))
        tok_copies[c].wait()

        @pl.loop(0, chunk // strip, unroll=4)
        def _(i):
            here = pl.ds(pl.multiple_of(c * chunk + i * strip, strip), strip)
            squares = jnp.zeros((strip, piece), F32)
            for k in range(width // piece):
                x = xt[here, pl.ds(k * piece, piece)].astype(F32)
                squares = squares + x * x
            mean_sq = jnp.sum(squares, axis=-1, keepdims=True) * (1.0 / width)
            scale = jnp.broadcast_to(lax.rsqrt(mean_sq + 1e-05), (strip, piece))
            for k in range(width // piece):
                cols = pl.ds(k * piece, piece)
                x = xt[here, cols].astype(F32) * scale
                xn[here, cols] = (
                    x.reshape(strip // 8, 8, piece) * gains[:, cols][None]
                ).reshape(strip, piece).astype(BF16)

        if c == chunks - 1:
            own_copies[0].wait()
            own_copies[1].wait()
            own_copies[3].wait()
            for d in range(1, n_rows):
                weight_copy(d, 0).wait()
                weight_copy(d, 1).wait()
        total = project(c * chunk, chunk, wkv_buf)
        cosine, sine = tables(c * chunk, chunk)
        here = pl.ds(mine + c * chunk, chunk)
        for h in range(kv_heads):
            kv[here, pl.ds(h * HEAD, HEAD)] = rotate(
                total[:, h * HEAD : (h + 1) * HEAD], cosine, sine
            )
        kv[here, pl.ds(kvw, kvw)] = total[:, kvw:].astype(BF16)
        if back:

            @pl.when(has_next)
            def _():
                hop(0, c).start()

    last = [(back - 1, c) for c in reversed(range(chunks))] if back else []

    own_copies[2].wait()
    for d in range(1, n_rows):
        weight_copy(d, 2).wait()
    part = min(rows, 2 * chunk)
    for step in reversed(range(rows // part)):
        for _ in range(min(1, len(relayed))):
            arrived(*relayed.pop(0))
        total = project(step * part, part, wq_buf)
        cosine, sine = tables(step * part, part)
        for h in range(kv_heads):
            for g in range(group):
                col = (h * group + g) * HEAD
                u = rotate(total[:, col : col + HEAD], cosine, sine)
                for t in range(part // TQ):
                    q[step * (part // TQ) + t, h, pl.ds(g * TQ, TQ), :] = u[
                        t * TQ : (t + 1) * TQ
                    ]
    for event in relayed:
        arrived(*event)

    factor = math.log2(math.e) / math.sqrt(HEAD)

    for t in reversed(range(tiles)):
        first = t * TQ
        begin = max(mine + first + TQ - span, 0)
        while last and (last[0][1] + 1) * chunk > begin:
            arrived(*last.pop(0))
        query_at = lax.broadcasted_iota(jnp.int32, (TQ, 1), 0) + (mine + first)
        key_at = lax.broadcasted_iota(jnp.int32, (1, span), 1) + begin
        visible = (qdoc[pl.ds(first, TQ), :][:, :1] == kdoc[:, pl.ds(begin, span)]) & (
            query_at >= key_at
        )
        for h in range(kv_heads):
            keys = kv[pl.ds(begin, span), pl.ds(h * HEAD, HEAD)]
            vals = kv[pl.ds(begin, span), pl.ds(kvw + h * HEAD, HEAD)]
            s = lax.dot_general(
                q[t, h], keys, (((1,), (1,)), ((), ())), preferred_element_type=F32
            )
            s = jnp.where(visible[None], s.reshape(group, TQ, span), -1e30)
            p = jnp.exp2((s - jnp.max(s, axis=-1, keepdims=True)) * factor)
            total = jnp.sum(p, axis=-1, keepdims=True)
            mixed = jnp.dot(
                p.astype(BF16).reshape(group * TQ, span), vals, preferred_element_type=F32
            )
            mixed = (mixed.reshape(group, TQ, HEAD) / total).astype(BF16)
            for g in range(group):
                out[pl.ds(first, TQ), pl.ds((h * group + g) * HEAD, HEAD)] = mixed[g]
    for event in last:
        arrived(*event)

    for s in range(back):
        for c in range(chunks):

            @pl.when((at >= s) & has_next)
            def _():
                hop(s, c).wait_send()


def solution(mesh):
    n_rows = mesh.shape["rows"]
    n_attn = mesh.shape["attn"]

    def on_device(tokens, norm_gain, w_query, w_key, w_value, documents):
        rows, width = tokens.shape
        depth, qw = w_query.shape
        kvw = w_key.shape[1]
        back = min(n_attn - 1, -(-(MOST - 1) // rows))
        chunk = min(rows, TQ)
        chunks = rows // chunk
        table = jnp.asarray(rotary_table(documents.shape[1]))
        anywhere = pl.BlockSpec(memory_space=pl.ANY)
        vmem = pl.BlockSpec(memory_space=pltpu.VMEM)
        keys = (back + 1) * rows
        group = qw // kvw
        return pl.pallas_call(
            functools.partial(kernel, n_rows, n_attn, back, chunk),
            out_shape=jax.ShapeDtypeStruct((rows, qw), BF16),
            in_specs=[anywhere, vmem, anywhere, anywhere, anywhere, vmem, anywhere],
            out_specs=vmem,
            scratch_shapes=[
                pltpu.VMEM((8, width), F32),
                pltpu.VMEM((rows, width), BF16),
                pltpu.VMEM((rows, width), BF16),
                pltpu.VMEM((n_rows, depth, 2 * kvw), BF16),
                pltpu.VMEM((n_rows, depth, qw), BF16),
                pltpu.VMEM((keys, 2 * kvw), BF16),
                pltpu.VMEM((rows // TQ, kvw // HEAD, group * TQ, HEAD), BF16),
                pltpu.VMEM((rows, HEAD), F32),
                pltpu.VMEM((1, keys), jnp.int32),
                pltpu.VMEM((rows, TQ), jnp.int32),
                pltpu.SemaphoreType.DMA((chunks,)),
                pltpu.SemaphoreType.DMA((4,)),
                pltpu.SemaphoreType.DMA((n_rows, 3)),
                pltpu.SemaphoreType.DMA((n_rows, 3)),
                pltpu.SemaphoreType.DMA((max(back, 1), chunks)),
                pltpu.SemaphoreType.DMA((max(back, 1), chunks)),
            ],
            compiler_params=pltpu.CompilerParams(
                collective_id=0, has_side_effects=True, vmem_limit_bytes=60 << 20
            ),
            name="layer",
        )(tokens, norm_gain, w_query, w_key, w_value, documents, table)

    placed = (
        P(("rows", "attn"), None),
        P(),
        P("rows", "tp"),
        P("rows", "tp"),
        P("rows", "tp"),
        P("rows", None),
    )
    return jax.shard_map(
        on_device, mesh=mesh, in_specs=placed, out_specs=P(("rows", "attn"), "tp"), check_vma=False
    )
```
